32 devices in a mesh: dp: 16 (over z, y, x), tensor: 2 (over core).
Axes of the slice: x: 2, y: 2, z: 4, core: 2. Of those that a mesh axis runs over, the one named last changes fastest.
Arguments:
- hidden_in: bfloat16 [10240, 640], P(('dp', 'tensor')), may hold values from -6 to 6
- cotangent: bfloat16 [10240, 640], P(('dp', 'tensor')), may hold values from -6 to 6
- segment_ids: int32 [16, 640], P('dp'), may hold values from 0 to 3, never falling along the last dimension, each value on 1 to 560 neighbouring positions
- norm_gains: float32 [4, 640], P(None, 'dp'), may hold values from -0.6 to 0.6
- norm_first: float32 [4, 640], P(None, 'dp'), may hold values from -192 to 192
- norm_second: float32 [4, 640], P(None, 'dp'), may hold values from 25.6 to 409.6
- head_gains: float32 [2, 256], P(None, 'dp'), may hold values from -0.75 to 0.75
- head_first: float32 [2, 256], P(None, 'dp'), may hold values from -192 to 192
- head_second: float32 [2, 256], P(None, 'dp'), may hold values from 25.6 to 409.6
- query_weight: float32 [640, 1024], P('dp', 'tensor'), may hold values from -0.25 to 0.25
- query_first: float32 [640, 1024], P('dp', 'tensor'), may hold values from -192 to 192
- query_second: float32 [640, 1024], P('dp', 'tensor'), may hold values from 25.6 to 409.6
- kv_weight: float32 [640, 512], P('dp'), may hold values from -0.25 to 0.25
- kv_first: float32 [640, 512], P('dp'), may hold values from -192 to 192
- kv_second: float32 [640, 512], P('dp'), may hold values from 25.6 to 409.6
- out_weight: float32 [1024, 640], P('tensor', 'dp'), may hold values from -0.1875 to 0.1875
- out_first: float32 [1024, 640], P('tensor', 'dp'), may hold values from -192 to 192
- out_second: float32 [1024, 640], P('tensor', 'dp'), may hold values from 25.6 to 409.6
- gate_up_weight: float32 [640, 2, 2048], P('dp', None, 'tensor'), may hold values from -0.25 to 0.25
- gate_up_first: float32 [640, 2, 2048], P('dp', None, 'tensor'), may hold values from -192 to 192
- gate_up_second: float32 [640, 2, 2048], P('dp', None, 'tensor'), may hold values from 25.6 to 409.6
- down_weight: float32 [2048, 640], P('tensor', 'dp'), may hold values from -0.125 to 0.125
- down_first: float32 [2048, 640], P('tensor', 'dp'), may hold values from -192 to 192
- down_second: float32 [2048, 640], P('tensor', 'dp'), may hold values from 25.6 to 409.6
Outputs:
- layer_out: bfloat16 [10240, 640], P(('dp', 'tensor'))
- input_grad: bfloat16 [10240, 640], P(('dp', 'tensor'))
- norm_grad: float32 [4, 640], P(None, 'dp')
- head_grad: float32 [2, 256], P(None, 'dp')
- query_grad: float32 [640, 1024], P('dp', 'tensor')
- kv_grad: float32 [640, 512], P('dp')
- out_grad: float32 [1024, 640], P('tensor', 'dp')
- gate_up_grad: float32 [640, 2, 2048], P('dp', None, 'tensor')
- down_grad: float32 [2048, 640], P('tensor', 'dp')
- new_norm_gains: float32 [4, 640], P(None, 'dp')
- new_norm_first: float32 [4, 640], P(None, 'dp')
- new_norm_second: float32 [4, 640], P(None, 'dp')
- new_head_gains: float32 [2, 256], P(None, 'dp')
- new_head_first: float32 [2, 256], P(None, 'dp')
- new_head_second: float32 [2, 256], P(None, 'dp')
- new_query_weight: float32 [640, 1024], P('dp', 'tensor')
- new_query_first: float32 [640, 1024], P('dp', 'tensor')
- new_query_second: float32 [640, 1024], P('dp', 'tensor')
- new_kv_weight: float32 [640, 512], P('dp')
- new_kv_first: float32 [640, 512], P('dp')
- new_kv_second: float32 [640, 512], P('dp')
- new_out_weight: float32 [1024, 640], P('tensor', 'dp')
- new_out_first: float32 [1024, 640], P('tensor', 'dp')
- new_out_second: float32 [1024, 640], P('tensor', 'dp')
- new_gate_up_weight: float32 [640, 2, 2048], P('dp', None, 'tensor')
- new_gate_up_first: float32 [640, 2, 2048], P('dp', None, 'tensor')
- new_gate_up_second: float32 [640, 2, 2048], P('dp', None, 'tensor')
- new_down_weight: float32 [2048, 640], P('tensor', 'dp')
- new_down_first: float32 [2048, 640], P('tensor', 'dp')
- new_down_second: float32 [2048, 640], P('tensor', 'dp')
The draws below stay inside these ranges and needn't reach their ends.
Inputs may be any that keep to these rules, and one draw needn't show every extreme that they name: `segment_ids`: segment numbers never fall along a group's 640 tokens; each of the 4 segments of a group holds 1 to 560 tokens, and some segment holds exactly 560.
All inputs are finite; a program needn't handle non-finite values.
Results may differ from the reference program's by a relative error of at most 0.025.
Values may be sent and summed in bfloat16 or wider, within the bound.
No kernel may reach another device: no remote copies, remote signals or barrier semaphores. Data moves between devices by JAX's collectives and lax.ppermute only.
A program may use at most 128 MiB of HBM per device.

```python
import math
from functools import partial
import jax
import jax.numpy as jnp
import numpy as np
from jax import lax

D = 640
HEADS = 4
HD = 256
FF = 2048
WINDOW = 512
TOK_DEV = 640
SEQS = 4
LMAX = 560
TOKENS = 10240
N_DP = 16
N_TENSOR = 2


def level_of(stream_key, dims, cuts, low, top_value):
    level = 1.0
    for dim, parts in cuts:
        steps = jax.random.uniform(jax.random.fold_in(jax.random.fold_in(stream_key, 6), dim), (parts,), jnp.float32, low / len(cuts), top_value / len(cuts))
        level = level * jnp.repeat(jnp.exp(steps), dims[dim] // parts).reshape((-1,) + (1,) * (len(dims) - 1 - dim))
    return level


def split_up(amount, total, most, skew):
    weights = [(1 << 20) // math.isqrt(standing ** skew) + 1 for standing in range(2, amount + 1)]
    rest, given = total - most - (amount - 1), [1] * (amount - 1)
    while rest > 0:
        candidates = [i for i in range(amount - 1) if given[i] < most]
        whole, budget = sum([weights[i] for i in candidates]), rest
        for i in candidates:
            more = min(most - given[i], max(1, budget * weights[i] // whole), rest)
            given[i] = given[i] + more
            rest = rest - more
    return np.array([most] + given)


def uneven(rng, amount, total, limit, skew):
    if amount == 2:
        one = jax.random.randint(rng, (), max(1, total - limit), min(limit, total - 1) + 1)
        return jnp.stack([one, total - one])
    tallies = jnp.asarray(split_up(amount, total, limit, skew), jnp.int32)
    twos = (amount - 1) // 2
    giver, receiver = tallies[1:1 + 2 * twos:2], tallies[2:2 + 2 * twos:2]
    slack = jnp.minimum(giver - 1, limit - receiver)
    moved = jax.random.randint(jax.random.fold_in(rng, 1), (twos,), 0, 1 << 20) % (slack + 1)
    tallies = tallies.at[1:1 + 2 * twos:2].set(giver - moved).at[2:2 + 2 * twos:2].set(receiver + moved)
    return tallies[jax.random.permutation(jax.random.fold_in(rng, 2), amount)]


def scatter_about(own_key, extent, scale, limit, split=(), kind=jnp.bfloat16):
    entries = scale * jax.random.normal(own_key, extent, jnp.float32)
    if split:
        entries = entries * level_of(own_key, extent, split, -0.22, 0.18)
    return jnp.clip(entries, -limit, limit).astype(kind)


def setup_inputs(seed: int = 0) -> dict:
    arg_keys = jax.random.split(jax.random.key(seed), 25)
    hidden_in = scatter_about(arg_keys[0], (TOKENS, D), 1.0, 6.0, ((0, 32),))
    cotangent = scatter_about(arg_keys[1], (TOKENS, D), 1.0, 6.0, ((0, 32),))
    segment_ids = jax.vmap(lambda own: jnp.searchsorted(jnp.cumsum(uneven(own, SEQS, TOK_DEV, LMAX, 2)), jnp.arange(TOK_DEV), side="right"))(jax.random.split(arg_keys[2], N_DP)).reshape((N_DP, TOK_DEV)).astype(jnp.int32)
    norm_gains = scatter_about(arg_keys[3], (4, D), 0.15, 0.6, ((1, 16),), jnp.float32)
    norm_first = scatter_about(arg_keys[4], (4, D), (0.3 * TOKENS ** 0.5), 192.0, ((1, 16),), jnp.float32)
    norm_second = jnp.clip(jnp.exp(math.log(409.6) - 2.7725887 * jax.random.uniform(arg_keys[5], (4, D), jnp.float32) ** level_of(arg_keys[5], (4, D), ((1, 16),), -0.2, 0.2)), 25.6, 409.6)
    head_gains = scatter_about(arg_keys[6], (2, HD), 0.25, 0.75, ((1, 16),), jnp.float32)
    head_first = scatter_about(arg_keys[7], (2, HD), (0.3 * TOKENS ** 0.5), 192.0, ((1, 16),), jnp.float32)
    head_second = jnp.clip(jnp.exp(math.log(409.6) - 2.7725887 * jax.random.uniform(arg_keys[8], (2, HD), jnp.float32) ** level_of(arg_keys[8], (2, HD), ((1, 16),), -0.2, 0.2)), 25.6, 409.6)
    query_weight = scatter_about(arg_keys[9], (D, HEADS * HD), D ** -0.5, 0.25, ((0, 16), (1, 2)), jnp.float32)
    query_first = scatter_about(arg_keys[10], (D, HEADS * HD), (0.3 * TOKENS ** 0.5), 192.0, ((0, 16), (1, 2)), jnp.float32)
    query_second = jnp.clip(jnp.exp(math.log(409.6) - 2.7725887 * jax.random.uniform(arg_keys[11], (D, HEADS * HD), jnp.float32) ** level_of(arg_keys[11], (D, HEADS * HD), ((0, 16), (1, 2)), -0.2, 0.2)), 25.6, 409.6)
    kv_weight = scatter_about(arg_keys[12], (D, 2 * HD), D ** -0.5, 0.25, ((0, 16),), jnp.float32)
    kv_first = scatter_about(arg_keys[13], (D, 2 * HD), (0.3 * TOKENS ** 0.5), 192.0, ((0, 16),), jnp.float32)
    kv_second = jnp.clip(jnp.exp(math.log(409.6) - 2.7725887 * jax.random.uniform(arg_keys[14], (D, 2 * HD), jnp.float32) ** level_of(arg_keys[14], (D, 2 * HD), ((0, 16),), -0.2, 0.2)), 25.6, 409.6)
    out_weight = scatter_about(arg_keys[15], (HEADS * HD, D), (HEADS * HD) ** -0.5, 0.1875, ((0, 2), (1, 16)), jnp.float32)
    out_first = scatter_about(arg_keys[16], (HEADS * HD, D), (0.3 * TOKENS ** 0.5), 192.0, ((0, 2), (1, 16)), jnp.float32)
    out_second = jnp.clip(jnp.exp(math.log(409.6) - 2.7725887 * jax.random.uniform(arg_keys[17], (HEADS * HD, D), jnp.float32) ** level_of(arg_keys[17], (HEADS * HD, D), ((0, 2), (1, 16)), -0.2, 0.2)), 25.6, 409.6)
    gate_up_weight = scatter_about(arg_keys[18], (D, 2, FF), D ** -0.5, 0.25, ((0, 16), (2, 2)), jnp.float32)
    gate_up_first = scatter_about(arg_keys[19], (D, 2, FF), (0.3 * TOKENS ** 0.5), 192.0, ((0, 16), (2, 2)), jnp.float32)
    gate_up_second = jnp.clip(jnp.exp(math.log(409.6) - 2.7725887 * jax.random.uniform(arg_keys[20], (D, 2, FF), jnp.float32) ** level_of(arg_keys[20], (D, 2, FF), ((0, 16), (2, 2)), -0.2, 0.2)), 25.6, 409.6)
    down_weight = scatter_about(arg_keys[21], (FF, D), FF ** -0.5, 0.125, ((0, 2), (1, 16)), jnp.float32)
    down_first = scatter_about(arg_keys[22], (FF, D), (0.3 * TOKENS ** 0.5), 192.0, ((0, 2), (1, 16)), jnp.float32)
    down_second = jnp.clip(jnp.exp(math.log(409.6) - 2.7725887 * jax.random.uniform(arg_keys[23], (FF, D), jnp.float32) ** level_of(arg_keys[23], (FF, D), ((0, 2), (1, 16)), -0.2, 0.2)), 25.6, 409.6)
    return dict(hidden_in=hidden_in, cotangent=cotangent, segment_ids=segment_ids, norm_gains=norm_gains, norm_first=norm_first, norm_second=norm_second, head_gains=head_gains, head_first=head_first, head_second=head_second, query_weight=query_weight, query_first=query_first, query_second=query_second, kv_weight=kv_weight, kv_first=kv_first, kv_second=kv_second, out_weight=out_weight, out_first=out_first, out_second=out_second, gate_up_weight=gate_up_weight, gate_up_first=gate_up_first, gate_up_second=gate_up_second, down_weight=down_weight, down_first=down_first, down_second=down_second)


eps_norm = 1e-06
rope_base = 10000.0
beta_one = 0.9
beta_two = 0.95
adam_eps = 1e-08
learn_rate = 0.02
decay_rate = 0.01
step_count = 4.0

def rms_norm(value, gain):
    return value * lax.rsqrt(lax.optimization_barrier(jnp.mean(value * value, axis=-1, keepdims=True)) + eps_norm) * (1.0 + gain)

def glu(gate, up):
    return jax.nn.gelu(gate, approximate=True) * up

def positions_and_mask(segments):
    count = segments.shape[0]
    index = jnp.arange(count, dtype=jnp.int32)
    change = jnp.concatenate([jnp.ones((1,), dtype=jnp.bool_), segments[1:] != segments[:-1]])
    start = lax.cummax(jnp.where(change, index, jnp.zeros_like(index)), axis=0)
    position = index - start
    allowed = (segments[:, None] == segments[None, :]) & (index[None, :] <= index[:, None]) & (index[:, None] - index[None, :] < WINDOW)
    return (position, allowed)

def rope_tables(position, width):
    half = width // 2
    freqs = rope_base ** (-2.0 * jnp.arange(half, dtype=jnp.float32) / width)
    angle = position.astype(jnp.float32)[:, None] * freqs[None, :]
    angle = jnp.concatenate([angle, angle], axis=1)
    return (jnp.cos(angle)[:, None, :], jnp.sin(angle)[:, None, :])

def head_prepare(value, gain, cosine, sine):
    normal = rms_norm(value, gain)
    half = normal.shape[-1] // 2
    turned = jnp.concatenate([-normal[..., half:], normal[..., :half]], axis=-1)
    return normal * cosine + turned * sine

def attend(query16, key16, value16, allowed):
    scale = query16.shape[-1] ** (-0.5)
    scores = jnp.einsum('ihd,jd->hij', query16.astype(jnp.float32), key16.astype(jnp.float32)) * scale
    scores = jnp.where(allowed[None], scores, -1e+30)
    peak = lax.optimization_barrier(jnp.max(scores, axis=-1, keepdims=True))
    total = lax.optimization_barrier(jnp.sum(jnp.exp(scores - peak), axis=-1, keepdims=True))
    logsum = peak + jnp.log(total)
    probs = jnp.exp(scores - logsum).astype(jnp.bfloat16)
    mixed = jnp.einsum('hij,jd->ihd', probs.astype(jnp.float32), value16.astype(jnp.float32)).astype(jnp.bfloat16)
    return (mixed, logsum)

def attend_back(query16, key16, value16, allowed, mixed16, logsum, grad16):
    scale = query16.shape[-1] ** (-0.5)
    scores = jnp.einsum('ihd,jd->hij', query16.astype(jnp.float32), key16.astype(jnp.float32)) * scale
    scores = jnp.where(allowed[None], scores, -1e+30)
    probs32 = jnp.exp(scores - logsum)
    probs16 = probs32.astype(jnp.bfloat16)
    grad32 = grad16.astype(jnp.float32)
    delta = jnp.einsum('ihd,ihd->hi', grad32, mixed16.astype(jnp.float32))
    grad_value = jnp.einsum('hij,ihd->jd', probs16.astype(jnp.float32), grad32)
    grad_probs = jnp.einsum('ihd,jd->hij', grad32, value16.astype(jnp.float32))
    grad_scores = (probs32 * (grad_probs - delta[:, :, None]) * scale).astype(jnp.bfloat16)
    grad_query = jnp.einsum('hij,jd->ihd', grad_scores.astype(jnp.float32), key16.astype(jnp.float32))
    grad_key = jnp.einsum('hij,ihd->jd', grad_scores.astype(jnp.float32), query16.astype(jnp.float32))
    return (grad_query, grad_key, grad_value)

def adamw(weight, first, second, grad):
    new_first = beta_one * first + (1.0 - beta_one) * grad
    new_second = beta_two * second + (1.0 - beta_two) * grad * grad
    update = new_first / (1.0 - beta_one ** step_count) / (jnp.sqrt(new_second / (1.0 - beta_two ** step_count)) + adam_eps)
    return (weight - learn_rate * (update + decay_rate * weight), new_first, new_second)

def rounded(weight):
    return lax.optimization_barrier(weight.astype(jnp.bfloat16))

def reference(hidden_in, cotangent, segment_ids, norm_gains, norm_first, norm_second, head_gains, head_first, head_second, query_weight, query_first, query_second, kv_weight, kv_first, kv_second, out_weight, out_first, out_second, gate_up_weight, gate_up_first, gate_up_second, down_weight, down_first, down_second):
    gains = rounded(norm_gains).astype(jnp.float32)
    head_gain = rounded(head_gains).astype(jnp.float32)
    query16 = rounded(query_weight)
    keyval16 = rounded(kv_weight)
    output16 = rounded(out_weight)
    gate16 = rounded(gate_up_weight).reshape(D, 2 * FF)
    down16 = rounded(down_weight)
    per_half = HEADS // N_TENSOR

    def one_group(grads, group):
        rows_in, rows_cot, segments = group
        position, allowed = positions_and_mask(segments)
        cosine, sine = rope_tables(position, HD)
        input32 = rows_in.astype(jnp.float32)
        normed = rms_norm(input32, gains[0]).astype(jnp.bfloat16)
        query = jnp.dot(normed, query16, preferred_element_type=jnp.float32).reshape(TOK_DEV, HEADS, HD)
        keyval = jnp.dot(normed, keyval16, preferred_element_type=jnp.float32)
        key_pre = keyval[:, None, :HD]
        query_rot = head_prepare(query, head_gain[0], cosine, sine).astype(jnp.bfloat16)
        key_rot = head_prepare(key_pre, head_gain[1], cosine, sine)[:, 0].astype(jnp.bfloat16)
        values = keyval[:, HD:].astype(jnp.bfloat16)
        mixed, logsum = attend(query_rot, key_rot, values, allowed)
        mixed_flat = mixed.reshape(TOK_DEV, HEADS * HD)
        attn = jnp.dot(mixed_flat, output16, preferred_element_type=jnp.float32)
        resid = input32 + rms_norm(attn, gains[1])
        hidden_normed = rms_norm(resid, gains[2]).astype(jnp.bfloat16)
        gate_up = jnp.dot(hidden_normed, gate16, preferred_element_type=jnp.float32).reshape(TOK_DEV, 2, FF)
        active = glu(gate_up[:, 0], gate_up[:, 1]).astype(jnp.bfloat16)
        ffn = jnp.dot(active, down16, preferred_element_type=jnp.float32)
        layer_out = (resid + rms_norm(ffn, gains[3])).astype(jnp.bfloat16)
        grad_out = rows_cot.astype(jnp.float32)
        unused, pull = jax.vjp(rms_norm, ffn, gains[3])
        grad_ffn, grad_g3 = pull(grad_out)
        grad_ffn16 = grad_ffn.astype(jnp.bfloat16)
        grad_active = jnp.dot(grad_ffn16, down16.T, preferred_element_type=jnp.float32)
        down_grad = jnp.dot(active.T, grad_ffn16, preferred_element_type=jnp.float32)
        unused, pull = jax.vjp(glu, gate_up[:, 0], gate_up[:, 1])
        grad_gate, grad_up = pull(grad_active)
        grad_gateup = jnp.stack([grad_gate, grad_up], axis=1).astype(jnp.bfloat16).reshape(TOK_DEV, 2 * FF)
        gate_grad = jnp.dot(hidden_normed.T, grad_gateup, preferred_element_type=jnp.float32).reshape(D, 2, FF)
        grad_hidden = jnp.dot(grad_gateup, gate16.T, preferred_element_type=jnp.float32)
        unused, pull = jax.vjp(rms_norm, resid, gains[2])
        grad_back, grad_g2 = pull(grad_hidden)
        grad_resid = grad_out + grad_back
        unused, pull = jax.vjp(rms_norm, attn, gains[1])
        grad_attn, grad_g1 = pull(grad_resid)
        grad_attn16 = grad_attn.astype(jnp.bfloat16)
        grad_mixed = jnp.dot(grad_attn16, output16.T, preferred_element_type=jnp.float32).astype(jnp.bfloat16).reshape(TOK_DEV, HEADS, HD)
        out_grad = jnp.dot(mixed_flat.T, grad_attn16, preferred_element_type=jnp.float32)
        prepare = partial(head_prepare, cosine=cosine, sine=sine)
        query_parts = []
        kv_grad = jnp.zeros((D, 2 * HD), jnp.float32)
        grad_normed = jnp.zeros((TOK_DEV, D), jnp.float32)
        head_grad = jnp.zeros((2, HD), jnp.float32)
        for half in range(N_TENSOR):
            lower = half * per_half
            upper = lower + per_half
            grad_qrot, grad_krot, grad_vals = attend_back(query_rot[:, lower:upper], key_rot, values, allowed, mixed[:, lower:upper], logsum[lower:upper], grad_mixed[:, lower:upper])
            unused, pull = jax.vjp(prepare, query[:, lower:upper], head_gain[0])
            grad_q, grad_gq = pull(grad_qrot)
            unused, pull = jax.vjp(prepare, key_pre, head_gain[1])
            grad_k, grad_gk = pull(grad_krot[:, None, :])
            query_parts.append(grad_q.astype(jnp.bfloat16))
            grad_keyval = jnp.concatenate([grad_k[:, 0], grad_vals], axis=1).astype(jnp.bfloat16)
            kv_grad = kv_grad + jnp.dot(normed.T, grad_keyval, preferred_element_type=jnp.float32)
            grad_normed = grad_normed + jnp.dot(grad_keyval, keyval16.T, preferred_element_type=jnp.float32)
            head_grad = head_grad + jnp.stack([grad_gq, grad_gk])
        grad_query16 = jnp.concatenate(query_parts, axis=1).reshape(TOK_DEV, HEADS * HD)
        query_grad = jnp.dot(normed.T, grad_query16, preferred_element_type=jnp.float32)
        grad_normed = grad_normed + jnp.dot(grad_query16, query16.T, preferred_element_type=jnp.float32)
        unused, pull = jax.vjp(rms_norm, input32, gains[0])
        grad_in, grad_g0 = pull(grad_normed)
        input_grad = (grad_resid + grad_in).astype(jnp.bfloat16)
        norm_grad = jnp.stack([grad_g0, grad_g1, grad_g2, grad_g3])
        terms = (norm_grad, head_grad, query_grad, kv_grad, out_grad, gate_grad, down_grad)
        new_grads = tuple((total + term for total, term in zip(grads, terms)))
        return (new_grads, (layer_out, input_grad))
    zeros = (jnp.zeros((4, D), jnp.float32), jnp.zeros((2, HD), jnp.float32), jnp.zeros((D, HEADS * HD), jnp.float32), jnp.zeros((D, 2 * HD), jnp.float32), jnp.zeros((HEADS * HD, D), jnp.float32), jnp.zeros((D, 2, FF), jnp.float32), jnp.zeros((FF, D), jnp.float32))
    groups = (hidden_in.reshape(N_DP, TOK_DEV, D), cotangent.reshape(N_DP, TOK_DEV, D), segment_ids)
    grads, (layer_out, input_grad) = lax.scan(one_group, zeros, groups)
    norm_grad, head_grad, query_grad, kv_grad, out_grad, gate_grad, down_grad = grads
    new_norm = adamw(norm_gains, norm_first, norm_second, norm_grad)
    new_head = adamw(head_gains, head_first, head_second, head_grad)
    new_query = adamw(query_weight, query_first, query_second, query_grad)
    new_keyval = adamw(kv_weight, kv_first, kv_second, kv_grad)
    new_output = adamw(out_weight, out_first, out_second, out_grad)
    new_gate = adamw(gate_up_weight, gate_up_first, gate_up_second, gate_grad)
    new_down = adamw(down_weight, down_first, down_second, down_grad)
    return (layer_out.reshape(TOKENS, D), input_grad.reshape(TOKENS, D), norm_grad, head_grad, query_grad, kv_grad, out_grad, gate_grad, down_grad, new_norm[0], new_norm[1], new_norm[2], new_head[0], new_head[1], new_head[2], new_query[0], new_query[1], new_query[2], new_keyval[0], new_keyval[1], new_keyval[2], new_output[0], new_output[1], new_output[2], new_gate[0], new_gate[1], new_gate[2], new_down[0], new_down[1], new_down[2])
```

```python
from functools import partial

import jax
import jax.numpy as jnp
from jax import lax
from jax.sharding import PartitionSpec as P

WINDOW = 512

eps_norm = 1e-06
rope_base = 10000.0
beta_one = 0.9
beta_two = 0.95
adam_eps = 1e-08
learn_rate = 0.02
decay_rate = 0.01
step_count = 4.0


f32 = jnp.float32
bf16 = jnp.bfloat16


def rms_norm(value, gain):
    return (
        value * lax.rsqrt(jnp.mean(value * value, axis=-1, keepdims=True) + eps_norm) * (1.0 + gain)
    )


def glu(gate, up):
    return jax.nn.gelu(gate, approximate=True) * up


def rope_tables(position, width):
    half = width // 2
    freqs = rope_base ** (-2.0 * jnp.arange(half, dtype=f32) / width)
    angle = position.astype(f32)[:, None] * freqs[None, :]
    cosine, sine = jnp.cos(angle), jnp.sin(angle)
    return (
        jnp.concatenate([cosine, cosine], axis=1)[:, None, :],
        jnp.concatenate([sine, sine], axis=1)[:, None, :],
    )


def head_prepare(value, gain, cosine, sine):
    normal = rms_norm(value, gain)
    half = normal.shape[-1] // 2
    turned = jnp.concatenate([-normal[..., half:], normal[..., :half]], axis=-1)
    return normal * cosine + turned * sine


def attend(query16, key16, value16, allowed):
    scale = query16.shape[-1] ** (-0.5)
    scores = jnp.einsum("ihd,jd->hij", query16, key16, preferred_element_type=f32) * scale
    scores = jnp.where(allowed[None], scores, -1e30)
    peak = jnp.max(scores, axis=-1, keepdims=True)
    total = jnp.sum(jnp.exp(scores - peak), axis=-1, keepdims=True)
    logsum = peak + jnp.log(total)
    probs = jnp.exp(scores - logsum).astype(bf16)
    mixed = jnp.einsum("hij,jd->ihd", probs, value16, preferred_element_type=f32).astype(bf16)
    return (mixed, logsum)


def attend_back(query16, key16, value16, allowed, mixed16, logsum, grad16):
    scale = query16.shape[-1] ** (-0.5)
    scores = jnp.einsum("ihd,jd->hij", query16, key16, preferred_element_type=f32) * scale
    scores = jnp.where(allowed[None], scores, -1e30)
    probs32 = jnp.exp(scores - logsum)
    probs16 = probs32.astype(bf16)
    delta = jnp.einsum("ihd,ihd->hi", grad16.astype(f32), mixed16.astype(f32))
    grad_value = jnp.einsum("hij,ihd->jd", probs16, grad16, preferred_element_type=f32)
    grad_probs = jnp.einsum("ihd,jd->hij", grad16, value16, preferred_element_type=f32)
    grad_scores = (probs32 * (grad_probs - delta[:, :, None]) * scale).astype(bf16)
    grad_query = jnp.einsum("hij,jd->ihd", grad_scores, key16, preferred_element_type=f32)
    grad_key = jnp.einsum("hij,ihd->jd", grad_scores, query16, preferred_element_type=f32)
    return (grad_query, grad_key, grad_value)


def adamw(weight, first, second, grad):
    new_first = beta_one * first + (1.0 - beta_one) * grad
    new_second = beta_two * second + (1.0 - beta_two) * grad * grad
    update = (
        new_first
        / (1.0 - beta_one**step_count)
        / (jnp.sqrt(new_second / (1.0 - beta_two**step_count)) + adam_eps)
    )
    return (weight - learn_rate * (update + decay_rate * weight), new_first, new_second)


def contract_rows(left, right):
    return lax.dot_general(left, right, (((0,), (0,)), ((), ())), preferred_element_type=f32)


def matmul(left, right, right_dim=0):
    return lax.dot_general(
        left, right, (((1,), (right_dim,)), ((), ())), preferred_element_type=f32
    )


def swap(value):
    return lax.ppermute(value, "tensor", [(0, 1), (1, 0)])


def after(value, *anchors):
    return lax.optimization_barrier((value, *anchors))[0]


def both_rows(own):
    return jnp.concatenate([own, swap(own)], axis=0)


def scatter_product(pairs):
    rows = pairs[0][0].shape[0] // 2

    def part(lo):
        total = None
        for left, right, right_dim in pairs:
            piece = matmul(left[lo : lo + rows], right, right_dim)
            total = piece if total is None else total + piece
        return total

    sent = swap(part(rows).astype(bf16))
    return part(0) + sent.astype(f32)


class Grid:
    def __init__(self, mesh):
        self.size = mesh.shape["dp"]
        self.cube = self.size == 16
        if self.cube:
            self.z_perms = [[(i, (i + 4 * k) % 16) for i in range(16)] for k in (1, 2, 3)]
            self.x_perm = [(i, i ^ 1) for i in range(16)]
            self.y_perm = [(i, i ^ 2) for i in range(16)]

    def coords(self):
        i = lax.axis_index("dp")
        return i // 4, (i // 2) % 2, i % 2

    def gather(self, blocks, anchors=()):
        if not self.cube:
            return [lax.all_gather(b, "dp", axis=0, tiled=True) for b in blocks], ()
        z, y, x = self.coords()
        blocks = [after(b, *anchors) for b in blocks] if anchors else blocks
        outs, marks = [], []
        for block in blocks:
            r, c = block.shape
            moved = [lax.ppermute(block, "dp", p) for p in self.z_perms]
            marks.extend(moved)
            column = jnp.zeros((4, r, c), block.dtype)
            for k, piece in enumerate([block] + moved):
                column = lax.dynamic_update_slice(column, piece[None], ((z + 4 - k) % 4, 0, 0))
            by_x = lax.ppermute(column, "dp", self.x_perm)
            by_y = lax.ppermute(column, "dp", self.y_perm)
            diag_low = lax.ppermute(by_x[:2], "dp", self.y_perm)
            diag_high = lax.ppermute(by_y[2:], "dp", self.x_perm)
            out = jnp.zeros((4, 2, 2, r, c), block.dtype)
            put = lax.dynamic_update_slice
            out = put(out, column[:, None, None], (0, y, x, 0, 0))
            out = put(out, by_x[:, None, None], (0, y, 1 - x, 0, 0))
            out = put(out, by_y[:, None, None], (0, 1 - y, x, 0, 0))
            out = put(out, diag_low[:, None, None], (0, 1 - y, 1 - x, 0, 0))
            out = put(out, diag_high[:, None, None], (2, 1 - y, 1 - x, 0, 0))
            outs.append(out.reshape(16 * r, c))
        return outs, tuple(marks)

    def scatter(self, whole, wire):
        if not self.cube:
            return lax.psum_scatter(whole, "dp", scatter_dimension=0, tiled=True)
        z, y, x = self.coords()
        pick = lambda v, i, axis: lax.dynamic_index_in_dim(v, i, axis, keepdims=False)
        send = lambda v, perm: lax.ppermute(v.astype(wire), "dp", perm).astype(f32)
        n, c = whole.shape
        r, h = n // 16, c // 2
        grid = whole.reshape(4, 2, 2, r, c)
        left, right = grid[..., :h], grid[..., h:]
        left = pick(left, x, 2) + send(pick(left, 1 - x, 2), self.x_perm)
        right = pick(right, y, 1) + send(pick(right, 1 - y, 1), self.y_perm)
        left = pick(left, y, 1) + send(pick(left, 1 - y, 1), self.y_perm)
        right = pick(right, x, 1) + send(pick(right, 1 - x, 1), self.x_perm)
        column = jnp.concatenate([left, right], axis=-1)
        total = pick(column, z, 0)
        for k, perm in enumerate(self.z_perms):
            total = total + send(pick(column, (z + k + 1) % 4, 0), perm)
        return total


def body(
    grid,
    hidden_in,
    cotangent,
    segment_ids,
    norm_gains,
    norm_first,
    norm_second,
    head_gains,
    head_first,
    head_second,
    query_weight,
    query_first,
    query_second,
    kv_weight,
    kv_first,
    kv_second,
    out_weight,
    out_first,
    out_second,
    gate_up_weight,
    gate_up_first,
    gate_up_second,
    down_weight,
    down_first,
    down_second,
):
    n_dp = grid.size
    d_local = norm_gains.shape[1]
    h_local = head_gains.shape[1]
    q_width = query_weight.shape[1]
    ff_local = gate_up_weight.shape[2]
    small = jnp.zeros((8, 128), f32)
    small = small.at[:4, :d_local].set(norm_gains).at[4:6, :h_local].set(head_gains)
    qkv_block = jnp.concatenate([query_weight, kv_weight], axis=1).astype(bf16)
    out_block = out_weight.T.astype(bf16)
    gate_block = gate_up_weight[:, 0, :].astype(bf16)
    up_block = gate_up_weight[:, 1, :].astype(bf16)
    down_block = down_weight.T.astype(bf16)
    rows16 = both_rows(hidden_in)
    (small_full, qkv_full), mark = grid.gather([small.astype(bf16), qkv_block])
    (output_full,), mark = grid.gather([out_block], mark)
    (gate_full,), mark = grid.gather([gate_block], mark)
    (up_full,), mark = grid.gather([up_block], mark)
    (down_full,), mark = grid.gather([down_block], mark)
    small_full = small_full.reshape(n_dp, 8, 128).astype(f32)
    gains = small_full[:, :4, :d_local].transpose(1, 0, 2).reshape(4, -1)
    head_gain = small_full[:, 4:6, :h_local].transpose(1, 0, 2).reshape(2, -1)
    width = head_gain.shape[1]

    segments = segment_ids[0]
    count = segments.shape[0]
    index = jnp.arange(count, dtype=jnp.int32)
    start = jnp.sum((segments[None, :] < segments[:, None]).astype(jnp.int32), axis=1)
    first_core = lax.axis_index("tensor") == 0
    order = lambda v: jnp.where(first_core, v, jnp.roll(v, count // 2))
    segments, start, index = order(segments), order(start), order(index)
    allowed = (
        (segments[:, None] == segments[None, :])
        & (index[None, :] <= index[:, None])
        & (index[:, None] - index[None, :] < WINDOW)
    )
    cosine, sine = rope_tables(index - start, width)

    input32 = hidden_in.astype(f32)
    normed = rms_norm(rows16.astype(f32), gains[0]).astype(bf16)
    total_rows = count
    projected = matmul(normed, qkv_full)
    query = projected[:, :q_width].reshape(total_rows, -1, width)
    key_pre = projected[:, None, q_width : q_width + width]
    query_rot = head_prepare(query, head_gain[0], cosine, sine).astype(bf16)
    key_rot = head_prepare(key_pre, head_gain[1], cosine, sine)[:, 0].astype(bf16)
    values = projected[:, q_width + width :].astype(bf16)
    mixed, logsum = attend(query_rot, key_rot, values, allowed)
    mixed_flat = mixed.reshape(total_rows, -1)
    attn_part = scatter_product(((mixed_flat, output_full, 1),))
    resid = input32 + rms_norm(attn_part, gains[1])
    hidden_normed = both_rows(rms_norm(resid, gains[2]).astype(bf16))
    gate = matmul(hidden_normed, gate_full)
    up = matmul(hidden_normed, up_full)
    active = glu(gate, up).astype(bf16)
    ffn_part = scatter_product(((active, down_full, 1),))
    layer_out = (resid + rms_norm(ffn_part, gains[3])).astype(bf16)
    grad_out = cotangent.astype(f32)
    unused, pull = jax.vjp(rms_norm, ffn_part, gains[3])
    grad_ffn, grad_g3 = pull(grad_out)
    grad_ffn_full = both_rows(grad_ffn.astype(bf16))
    grad_active = matmul(grad_ffn_full, down_full)
    down_grad = grid.scatter(contract_rows(grad_ffn_full, active), bf16)
    unused, pull = jax.vjp(glu, gate, up)
    grad_gate, grad_up = pull(grad_active)
    grad_gate, grad_up = grad_gate.astype(bf16), grad_up.astype(bf16)
    gate_grad = grid.scatter(contract_rows(hidden_normed, grad_gate), bf16)
    up_grad = grid.scatter(contract_rows(hidden_normed, grad_up), bf16)
    grad_hidden = scatter_product(((grad_gate, gate_full, 1), (grad_up, up_full, 1)))
    unused, pull = jax.vjp(rms_norm, resid, gains[2])
    grad_back, grad_g2 = pull(grad_hidden)
    grad_resid = grad_out + grad_back
    unused, pull = jax.vjp(rms_norm, attn_part, gains[1])
    grad_attn, grad_g1 = pull(grad_resid)
    grad_attn_full = both_rows(grad_attn.astype(bf16))
    grad_mixed = matmul(grad_attn_full, output_full).astype(bf16)
    out_grad = grid.scatter(contract_rows(grad_attn_full, mixed_flat), bf16)
    grad_qrot, grad_krot, grad_values = attend_back(
        query_rot,
        key_rot,
        values,
        allowed,
        mixed,
        logsum,
        grad_mixed.reshape(total_rows, -1, width),
    )
    prepare = partial(head_prepare, cosine=cosine, sine=sine)
    unused, pull = jax.vjp(prepare, query, head_gain[0])
    grad_query, grad_gq = pull(grad_qrot)
    unused, pull = jax.vjp(prepare, key_pre, head_gain[1])
    grad_key, grad_gk = pull(grad_krot[:, None, :])
    grad_qkv16 = jnp.concatenate(
        [grad_query.reshape(total_rows, -1), grad_key[:, 0], grad_values], axis=1
    ).astype(bf16)
    qkv_grad = grid.scatter(contract_rows(normed, grad_qkv16), bf16)
    grad_normed = scatter_product(((grad_qkv16, qkv_full, 1),))
    unused, pull = jax.vjp(rms_norm, input32, gains[0])
    grad_in, grad_g0 = pull(grad_normed)
    input_grad = (grad_resid + grad_in).astype(bf16)
    norm_part = jnp.stack([grad_g0, grad_g1, grad_g2, grad_g3])
    head_part = jnp.stack([grad_gq, grad_gk])
    small_part = jnp.zeros((n_dp, 8, 128), f32)
    small_part = small_part.at[:, :4, :d_local].set(
        norm_part.reshape(4, n_dp, d_local).transpose(1, 0, 2)
    )
    small_part = small_part.at[:, 4:6, :h_local].set(
        head_part.reshape(2, n_dp, h_local).transpose(1, 0, 2)
    )
    small_grad = grid.scatter(small_part.reshape(n_dp * 8, 128), f32)
    small_grad = small_grad + swap(small_grad)
    norm_grad = small_grad[:4, :d_local]
    head_grad = small_grad[4:6, :h_local]
    query_grad = qkv_grad[:, :q_width]
    keyval_grad = qkv_grad[:, q_width:]
    keyval_grad = keyval_grad + swap(keyval_grad)
    gate_up_grad = jnp.stack([gate_grad, up_grad], axis=1)
    out_grad, down_grad = out_grad.T, down_grad.T
    new_norm = adamw(norm_gains, norm_first, norm_second, norm_grad)
    new_head = adamw(head_gains, head_first, head_second, head_grad)
    new_query = adamw(query_weight, query_first, query_second, query_grad)
    new_keyval = adamw(kv_weight, kv_first, kv_second, keyval_grad)
    new_output = adamw(out_weight, out_first, out_second, out_grad)
    new_gate = adamw(gate_up_weight, gate_up_first, gate_up_second, gate_up_grad)
    new_down = adamw(down_weight, down_first, down_second, down_grad)
    return (
        layer_out,
        input_grad,
        norm_grad,
        head_grad,
        query_grad,
        keyval_grad,
        out_grad,
        gate_up_grad,
        down_grad,
        *new_norm,
        *new_head,
        *new_query,
        *new_keyval,
        *new_output,
        *new_gate,
        *new_down,
    )


def solution(mesh):
    rows = P(("dp", "tensor"), None)
    vector = P(None, "dp")
    query = P("dp", "tensor")
    keyval = P("dp", None)
    turned = P("tensor", "dp")
    gate_up = P("dp", None, "tensor")
    states = (vector, vector, query, keyval, turned, gate_up, turned)
    placed = (rows, rows, P("dp", None)) + tuple(s for s in states for _ in range(3))
    return jax.shard_map(
        partial(body, Grid(mesh)),
        mesh=mesh,
        in_specs=placed,
        out_specs=(rows, rows) + states + tuple(s for s in states for _ in range(3)),
        check_vma=False,
    )
```
